32 devices in a mesh: groups: 2 (over y), dp: 4 (over z), net: 4 (over x, core).
Axes of the slice: x: 2, y: 2, z: 4, core: 2. Of those that a mesh axis runs over, the one named last changes fastest.
Arguments:
- part_emb: bfloat16 [8192, 512], P(('groups', 'dp', 'net')), parts along dimension 0, may hold values from -6 to 6
- assign: int32 [8192], P(('groups', 'dp', 'net')), parts along dimension 0, may hold values from 0 to 2047, as said below
- images: bfloat16 [4096, 512], P(('groups', 'dp', 'net')), parts along dimension 0, may hold values from -6 to 6
- negatives: int32 [32, 16], P('groups'), parts along dimension 0, may hold values from 0 to 1, as said below
Outputs:
- pair_loss: float32 [4096], P(('groups', 'dp', 'net')), parts along dimension 0
- net_grad: float32 [4096, 512], P(('groups', 'dp', 'net')), parts along dimension 0
- image_grad: float32 [4096, 512], P(('groups', 'dp', 'net')), parts along dimension 0
The draws below stay inside these ranges and needn't reach their ends.
There are 2 independent parts, one for each index of `groups`. The reference program is written for one: setup_inputs(seed, part) draws one part's arguments, and reference() takes and returns one part's arrays. A program takes and returns all parts, laid end to end along the dimension named above; each array names one. Nothing has to cross between parts.
Inputs may be any that keep to these rules, and one draw needn't show every extreme that they name: Partition i belongs to a pair of its own run: assign[i] // 512 == i // 1024; every pair has one partition or more. An entry 1 marks a column block used as hard negatives of a row block; counts differ widely between row blocks; every row block marks at least one column block of another run; the diagonal block is used whatever its entry.
All inputs are finite; a program needn't handle non-finite values.
Results may differ from the reference program's by a relative error of at most 0.005.
Values may be sent and summed in bfloat16 or wider, within the bound.
A program may use at most 64 MiB of HBM per device.

```python
import jax
import jax.numpy as jnp
from jax import lax

E = 512
BLOCK = 128
PAIR_DP = 512
PART_DP = 1024
PAIRS = 2048
PARTS_SIZE = 4096
NBLK = 16


def make_assign(key):
    base_key = jax.random.fold_in(key, 11)
    run_count = PAIRS // PAIR_DP

    def one_run(run_key, offset):
        fill_key, order_key = jax.random.split(run_key)
        spare_pairs = jax.random.randint(fill_key, (PART_DP - PAIR_DP,), 0, PAIR_DP).astype(jnp.int32)
        local_pairs = jnp.concatenate([jnp.arange(PAIR_DP, dtype=jnp.int32), spare_pairs])
        return jax.random.permutation(order_key, local_pairs) + offset
    run_keys = jax.random.split(base_key, run_count)
    offsets = jnp.arange(run_count, dtype=jnp.int32) * PAIR_DP
    return jax.vmap(one_run)(run_keys, offsets).reshape(PARTS_SIZE).astype(jnp.int32)


def block_shift(key):
    run_count = PAIRS // PAIR_DP
    run_step = jax.random.randint(jax.random.fold_in(key, 31), (), 1, run_count).astype(jnp.int32)
    return run_step * (PAIR_DP // BLOCK)


def bell_rows(key, count):
    return jnp.clip(jax.random.normal(key, (count, E), jnp.float32), -3.5, 3.5)


def draw_assign(key, part):
    return make_assign(key)


def draw_part_emb(key, part):
    assign = make_assign(key)
    latents = bell_rows(jax.random.fold_in(key, 21), PAIRS)
    noise = bell_rows(jax.random.fold_in(key, 22), PARTS_SIZE)
    rows = latents[assign] + 0.5 * noise
    return jnp.clip(rows, -6.0, 6.0).astype(jnp.bfloat16)


def draw_images(key, part):
    shift = block_shift(key)
    columns = jnp.arange(PAIRS, dtype=jnp.int32)
    twin_rows = (columns // BLOCK - shift) % NBLK * BLOCK + columns % BLOCK
    latents = bell_rows(jax.random.fold_in(key, 21), PAIRS)
    noise = bell_rows(jax.random.fold_in(key, 24), PAIRS)
    rows = latents + latents[twin_rows] + 0.5 * noise
    return jnp.clip(rows, -6.0, 6.0).astype(jnp.bfloat16)


def draw_negatives(key, part):
    level_key = jax.random.fold_in(key, 41)
    entry_key = jax.random.fold_in(key, 42)
    density_level = jax.random.randint(level_key, (NBLK, 1), 0, 6).astype(jnp.int32)
    entries = jax.random.randint(entry_key, (NBLK, NBLK), 0, 128).astype(jnp.int32)
    thresholds = jnp.left_shift(jnp.ones((NBLK, 1), jnp.int32), density_level)
    marked = (entries < thresholds).astype(jnp.int32)
    shift = block_shift(key)
    block_ids = jnp.arange(NBLK, dtype=jnp.int32)
    partner = ((block_ids[:, None] + shift) % NBLK == block_ids[None, :]).astype(jnp.int32)
    return jnp.maximum(marked, partner).astype(jnp.int32)


def setup_inputs(seed: int = 0, part: int = 0) -> dict:
    splits = jax.random.split(jax.random.key(seed), 5)
    own_keys = jax.random.split(jax.random.fold_in(splits[4], part), 5)
    return {
        "part_emb": draw_part_emb(jax.random.fold_in(jax.random.fold_in(splits[4], part), 71), part),
        "assign": draw_assign(jax.random.fold_in(jax.random.fold_in(splits[4], part), 71), part),
        "images": draw_images(jax.random.fold_in(jax.random.fold_in(splits[4], part), 71), part),
        "negatives": draw_negatives(jax.random.fold_in(jax.random.fold_in(splits[4], part), 71), part),
    }


logit_scale = 10.0

def unit_rows(matrix):
    squares = lax.optimization_barrier(jnp.sum(matrix * matrix, axis=1, keepdims=True))
    return (matrix * lax.rsqrt(squares + 1e-06)).astype(jnp.bfloat16)

def reference(part_emb, assign, images, negatives):
    pooled = jax.ops.segment_sum(part_emb.astype(jnp.float32), assign, num_segments=PAIRS)
    counted = jax.ops.segment_sum(jnp.ones((PARTS_SIZE,), jnp.float32), assign, num_segments=PAIRS)
    netlist_unit = unit_rows(pooled / counted[:, None]).astype(jnp.float32)
    image_unit = unit_rows(images.astype(jnp.float32)).astype(jnp.float32)
    live_blocks = jnp.maximum(negatives, jnp.eye(NBLK, dtype=jnp.int32)).astype(jnp.float32)

    def row_block(grad_images, block_index):
        first_row = (block_index * BLOCK).astype(jnp.int32)
        net_rows = lax.dynamic_slice_in_dim(netlist_unit, first_row, BLOCK, 0)
        own_images = lax.dynamic_slice_in_dim(image_unit, first_row, BLOCK, 0)
        block_mask = lax.dynamic_slice_in_dim(live_blocks, block_index, 1, 0)[0]
        column_mask = jnp.repeat(block_mask, BLOCK)
        logits = logit_scale * jnp.dot(net_rows, image_unit.T, precision=lax.Precision.HIGHEST)
        weights = jnp.exp(logits) * column_mask[None, :]
        totals = lax.optimization_barrier(jnp.sum(weights, axis=1))
        soft_weights = lax.optimization_barrier((weights / totals[:, None]).astype(jnp.bfloat16)).astype(jnp.float32)
        grad_rows = logit_scale * jnp.dot(soft_weights, image_unit, precision=lax.Precision.HIGHEST) - logit_scale * own_images
        grad_images = grad_images + logit_scale * jnp.dot(soft_weights.T, net_rows, precision=lax.Precision.HIGHEST)
        own_logit = logit_scale * lax.optimization_barrier(jnp.sum(net_rows * own_images, axis=1))
        pair_loss = jnp.log(totals) - own_logit
        return (grad_images, (pair_loss, grad_rows))
    start_grad = jnp.zeros((PAIRS, E), jnp.float32)
    block_ids = jnp.arange(NBLK).astype(jnp.int32)
    grad_images, (pair_loss, net_grad) = lax.scan(row_block, start_grad, block_ids)
    image_grad = grad_images - logit_scale * netlist_unit
    return (pair_loss.reshape(PAIRS), net_grad.reshape(PAIRS, E), image_grad)
```

```python
import functools

import jax
import jax.numpy as jnp
from jax import lax
from jax.experimental import pallas as pl
from jax.experimental.pallas import tpu as pltpu
from jax.sharding import PartitionSpec as P

BLOCK = 128
CHUNKS = 2
MESH = pl.DeviceIdType.MESH

logit_scale = 10.0


def each(count, body):
    if count <= 4:
        for k in range(1, count):
            body(k)
    else:

        def step(k, carry):
            body(k)
            return carry

        lax.fori_loop(1, count, step, 0)


def ordered_offset(k, size):
    if isinstance(k, int):
        return (k + 1) // 2 if k % 2 else size - k // 2
    return jnp.where(lax.rem(k, 2) == 1, lax.div(k + 1, 2), size - lax.div(k, 2))


def send(src, dst, send_sem, recv_sem, axis, peer):
    return pltpu.make_async_remote_copy(
        src_ref=src,
        dst_ref=dst,
        send_sem=send_sem,
        recv_sem=recv_sem,
        device_id={axis: peer},
        device_id_type=MESH,
    )


def kernel(
    net_size,
    dp_size,
    part_hbm,
    assign_ref,
    img_hbm,
    neg_ref,
    loss_ref,
    net_grad_ref,
    img_grad_ref,
    img_raw,
    part_all,
    assign_all,
    img_all,
    pooled,
    counted,
    unit,
    weights,
    soft,
    tot_all,
    total,
    row_out,
    row_in,
    col_out,
    col_in,
    local_sem,
    part_s,
    part_r,
    fwd_s,
    asg_s,
    asg_r,
    img_s,
    img_r,
    tot_s,
    tot_r,
    row_s,
    row_r,
    col_s,
    col_r,
):
    f32, bf16 = jnp.float32, jnp.bfloat16
    rows = img_raw.shape[0]
    part_rows = part_all.shape[1]
    chunk = part_rows // CHUNKS
    pair_dp = rows * net_size
    row_blocks = pair_dp // BLOCK
    own_blocks = rows // BLOCK
    chips = net_size // 2

    n = lax.axis_index("net")
    d = lax.axis_index("dp")
    core = lax.rem(n, 2)
    chip = lax.div(n, 2)
    sibling = n + 1 - 2 * core

    def net_peer(k):
        return lax.rem(n + k, net_size)

    def dp_peer(k):
        return lax.rem(d + k, dp_size)

    def chip_peer(k):
        return lax.rem(chip + k, chips)

    img_load = pltpu.make_async_copy(img_hbm, img_raw, local_sem.at[0])
    part_load = pltpu.make_async_copy(part_hbm, part_all.at[n], local_sem.at[1])
    img_load.start()
    part_load.start()

    barrier = pltpu.get_barrier_semaphore()
    each(
        net_size,
        lambda k: pl.semaphore_signal(
            barrier, inc=1, device_id={"net": net_peer(k)}, device_id_type=MESH
        ),
    )
    each(
        dp_size,
        lambda k: pl.semaphore_signal(
            barrier, inc=1, device_id={"dp": dp_peer(k)}, device_id_type=MESH
        ),
    )

    img_load.wait()
    h = img_raw[...].astype(f32)
    squares = jnp.sum(h * h, axis=1, keepdims=True)
    img_all[d] = (h * lax.rsqrt(squares + 1e-06)).astype(bf16)

    pl.semaphore_wait(barrier, net_size + dp_size - 2)

    def img_copy(k):
        off = ordered_offset(k, dp_size)
        return send(
            img_all.at[d], img_all.at[d], img_s.at[off], img_r.at[d], "dp", dp_peer(off)
        )

    def img_arrival(src):
        return send(img_all.at[src], img_all.at[src], img_s.at[0], img_r.at[src], "dp", d)

    def part_piece(ref, c):
        return ref.at[pl.ds(c * chunk, chunk)]

    def part_cross(k, c):
        return send(
            part_piece(part_hbm, c),
            part_piece(part_all.at[n], c),
            part_s.at[k, c],
            part_r.at[n, c],
            "net",
            chip_peer(k) * 2 + core,
        )

    def part_sibling(c):
        return send(
            part_piece(part_hbm, c),
            part_piece(part_all.at[n], c),
            part_s.at[0, c],
            part_r.at[n, c],
            "net",
            sibling,
        )

    def part_forward(k, c):
        origin = chip_peer(k) * 2 + core
        return send(
            part_piece(part_all.at[origin], c),
            part_piece(part_all.at[origin], c),
            fwd_s.at[k, c],
            part_r.at[origin, c],
            "net",
            sibling,
        )

    def part_arrival(origin, c):
        return send(
            part_piece(part_all.at[origin], c),
            part_piece(part_all.at[origin], c),
            part_s.at[0, c],
            part_r.at[origin, c],
            "net",
            sibling,
        )

    def asg_copy(k):
        return send(
            assign_ref, assign_all.at[n], asg_s.at[k], asg_r.at[n], "net", net_peer(k)
        )

    def asg_arrival(src):
        return send(
            assign_ref, assign_all.at[src], asg_s.at[0], asg_r.at[src], "net", sibling
        )

    each(net_size, lambda k: asg_copy(k).start())
    for c in range(CHUNKS):
        each(chips, lambda k: part_cross(k, c).start())
    each(dp_size, lambda k: img_copy(k).start())
    for c in range(CHUNKS):
        part_sibling(c).start()

    pair_ids = d * pair_dp + lax.broadcasted_iota(jnp.int32, (pair_dp, part_rows), 0)

    def pool(origin, assigned, first=False):
        member = (assigned == pair_ids).astype(f32)
        sums = jnp.dot(member.astype(bf16), part_all[origin], preferred_element_type=f32)
        counts = jnp.sum(member, axis=1, keepdims=True)
        if first:
            pooled[...] = sums
            counted[...] = counts
        else:
            pooled[...] += sums
            counted[...] += counts

    part_load.wait()
    pool(n, assign_ref[...], first=True)

    def pool_from(origin):
        asg_arrival(origin).wait_recv()
        pool(origin, assign_all[origin])

    for c in range(CHUNKS):
        part_arrival(sibling, c).wait_recv()
    pool_from(sibling)

    def pass_on(k):
        origin = chip_peer(k) * 2 + core
        for c in range(CHUNKS):
            part_arrival(origin, c).wait_recv()
            part_forward(k, c).start()
        pool_from(origin)

    each(chips, pass_on)

    def pool_passed(k):
        origin = chip_peer(k) * 2 + 1 - core
        for c in range(CHUNKS):
            part_arrival(origin, c).wait_recv()
        pool_from(origin)

    each(chips, pool_passed)

    p = pooled[...]
    cnt = counted[...]
    unit[...] = (
        p * lax.rsqrt(jnp.sum(p * p, axis=1, keepdims=True) + 1e-06 * (cnt * cnt))
    ).astype(bf16)

    def score(src):
        logits = logit_scale * lax.dot_general(
            img_all[src],
            unit[...],
            (((1,), (1,)), ((), ())),
            preferred_element_type=f32,
        )
        w = jnp.exp(logits)
        for q in range(own_blocks):
            column = (src * net_size + n) * own_blocks + q
            marks = []
            for b in range(row_blocks):
                row = d * row_blocks + b
                live = jnp.maximum(neg_ref[row, column], (row == column).astype(jnp.int32))
                marks.append(jnp.full((1, BLOCK), live.astype(f32), f32))
            masked = w[q * BLOCK : (q + 1) * BLOCK] * jnp.concatenate(marks, axis=1)
            start = pl.multiple_of(src * rows + q * BLOCK, BLOCK)
            weights[pl.ds(start, BLOCK), :] = masked
            tot_all[n] += jnp.sum(masked, axis=0, keepdims=True)

    tot_all[n] = jnp.zeros_like(tot_all[n])
    score(d)

    def score_from(k):
        src = dp_peer(ordered_offset(k, dp_size))
        img_arrival(src).wait_recv()
        score(src)

    each(dp_size, score_from)

    def tot_copy(k):
        return send(
            tot_all.at[n], tot_all.at[n], tot_s.at[k], tot_r.at[n], "net", net_peer(k)
        )

    def tot_arrival(src):
        return send(tot_all.at[src], tot_all.at[src], tot_s.at[0], tot_r.at[src], "net", sibling)

    each(net_size, lambda k: tot_copy(k).start())
    total[...] = tot_all[n]

    own = pl.ds(pl.multiple_of(n * rows, BLOCK), rows)
    own_logits = logit_scale * lax.dot_general(
        img_all[d], unit[own, :], (((1,), (1,)), ((), ())), preferred_element_type=f32
    )
    on_diagonal = lax.broadcasted_iota(jnp.int32, (rows, rows), 0) == lax.broadcasted_iota(
        jnp.int32, (rows, rows), 1
    )
    own_logit = jnp.sum(jnp.where(on_diagonal, own_logits, 0.0), axis=0, keepdims=True)

    def add_total(k):
        src = net_peer(k)
        tot_arrival(src).wait_recv()
        total[...] += tot_all[src]

    each(net_size, add_total)
    inverse = 1.0 / total[...]
    loss_ref[...] = jnp.log(total[:, own]) - own_logit

    def column_grad(src):
        span = pl.ds(pl.multiple_of(src * rows, BLOCK), rows)
        s = (weights[span, :] * inverse).astype(bf16)
        soft[span, :] = s
        return jnp.dot(s, unit[...], preferred_element_type=f32)

    def col_copy(k):
        off = ordered_offset(dp_size - k, dp_size)
        peer = dp_peer(off)
        return send(
            col_out.at[peer], col_in.at[d], col_s.at[off], col_r.at[d], "dp", peer
        )

    def col_arrival(src):
        return send(col_out.at[src], col_in.at[src], col_s.at[0], col_r.at[src], "dp", d)

    def column_send(k):
        peer = dp_peer(ordered_offset(dp_size - k, dp_size))
        col_out[peer] = column_grad(peer).astype(bf16)
        col_copy(k).start()

    each(dp_size, column_send)
    img_grad_ref[...] = column_grad(d) - unit[own, :].astype(f32)

    every_image = img_all[...].reshape(dp_size * rows, img_all.shape[2])

    def row_grad(dst):
        span = pl.ds(pl.multiple_of(dst * rows, BLOCK), rows)
        return lax.dot_general(
            soft[:, span], every_image, (((0,), (0,)), ((), ())), preferred_element_type=f32
        )

    def row_copy(k):
        peer = net_peer(k)
        return send(row_out.at[peer], row_in.at[n], row_s.at[k], row_r.at[n], "net", peer)

    def row_arrival(src):
        return send(row_out.at[src], row_in.at[src], row_s.at[0], row_r.at[src], "net", sibling)

    def row_send(k):
        peer = net_peer(k)
        row_out[peer] = row_grad(peer).astype(bf16)
        row_copy(k).start()

    each(net_size, row_send)
    net_grad_ref[...] = row_grad(n) - img_all[d].astype(f32)

    def row_add(k):
        src = net_peer(k)
        row_arrival(src).wait_recv()
        net_grad_ref[...] += row_in[src].astype(f32)

    each(net_size, row_add)
    net_grad_ref[...] = logit_scale * net_grad_ref[...]

    def col_add(k):
        src = dp_peer(ordered_offset(k, dp_size))
        col_arrival(src).wait_recv()
        img_grad_ref[...] += col_in[src].astype(f32)

    each(dp_size, col_add)
    img_grad_ref[...] = logit_scale * img_grad_ref[...]

    def net_done(k):
        asg_copy(k).wait_send()
        tot_copy(k).wait_send()
        row_copy(k).wait_send()

    def dp_done(k):
        img_copy(k).wait_send()
        col_copy(k).wait_send()

    each(net_size, net_done)
    each(dp_size, dp_done)
    for c in range(CHUNKS):
        part_sibling(c).wait_send()

        def chip_done(k):
            part_cross(k, c).wait_send()
            part_forward(k, c).wait_send()

        each(chips, chip_done)


def per_device(part_emb, assign, images, negatives):
    rows, width = images.shape
    part_rows = part_emb.shape[0]
    net_size = lax.axis_size("net")
    dp_size = lax.axis_size("dp")
    chips = net_size // 2
    pair_dp = rows * net_size
    columns = rows * dp_size
    f32, bf16 = jnp.float32, jnp.bfloat16
    dma = pltpu.SemaphoreType.DMA
    vmem = pl.BlockSpec(memory_space=pltpu.VMEM)
    smem = pl.BlockSpec(memory_space=pltpu.SMEM)
    hbm = pl.BlockSpec(memory_space=pl.ANY)
    loss, net_grad, img_grad = pl.pallas_call(
        functools.partial(kernel, net_size, dp_size),
        out_shape=(
            jax.ShapeDtypeStruct((1, rows), f32),
            jax.ShapeDtypeStruct((rows, width), f32),
            jax.ShapeDtypeStruct((rows, width), f32),
        ),
        in_specs=[hbm, vmem, hbm, smem],
        out_specs=(vmem, vmem, vmem),
        scratch_shapes=[
            pltpu.VMEM((rows, width), bf16),
            pltpu.VMEM((net_size, part_rows, width), bf16),
            pltpu.VMEM((net_size, 1, part_rows), jnp.int32),
            pltpu.VMEM((dp_size, rows, width), bf16),
            pltpu.VMEM((pair_dp, width), f32),
            pltpu.VMEM((pair_dp, 1), f32),
            pltpu.VMEM((pair_dp, width), bf16),
            pltpu.VMEM((columns, pair_dp), f32),
            pltpu.VMEM((columns, pair_dp), bf16),
            pltpu.VMEM((net_size, 1, pair_dp), f32),
            pltpu.VMEM((1, pair_dp), f32),
            pltpu.VMEM((net_size, rows, width), bf16),
            pltpu.VMEM((net_size, rows, width), bf16),
            pltpu.VMEM((dp_size, rows, width), bf16),
            pltpu.VMEM((dp_size, rows, width), bf16),
            dma((2,)),
            dma((chips, CHUNKS)),
            dma((net_size, CHUNKS)),
            dma((chips, CHUNKS)),
            dma((net_size,)),
            dma((net_size,)),
            dma((dp_size,)),
            dma((dp_size,)),
            dma((net_size,)),
            dma((net_size,)),
            dma((net_size,)),
            dma((net_size,)),
            dma((dp_size,)),
            dma((dp_size,)),
        ],
        compiler_params=pltpu.CompilerParams(
            collective_id=0, has_side_effects=True, vmem_limit_bytes=48 * 2**20
        ),
    )(part_emb, assign.reshape(1, part_rows), images, negatives)
    return loss.reshape(rows), net_grad, img_grad


def solution(mesh):
    in_specs = (
        P(("groups", "dp", "net"), None),
        P(("groups", "dp", "net")),
        P(("groups", "dp", "net"), None),
        P("groups", None),
    )
    out_specs = (
        P(("groups", "dp", "net")),
        P(("groups", "dp", "net"), None),
        P(("groups", "dp", "net"), None),
    )
    return jax.shard_map(
        per_device, mesh=mesh, in_specs=in_specs, out_specs=out_specs, check_vma=False
    )
```

```python
import functools

import jax
import jax.numpy as jnp
from jax import lax
from jax.experimental import pallas as pl
from jax.experimental.pallas import tpu as pltpu
from jax.sharding import PartitionSpec as P

BLOCK = 128
CHUNKS = 2
MESH = pl.DeviceIdType.MESH

logit_scale = 10.0


def each(count, body):
    if count <= 4:
        for k in range(1, count):
            body(k)
    else:

        def step(k, carry):
            body(k)
            return carry

        lax.fori_loop(1, count, step, 0)


def line_peer(k, d, size):
    surplus = jnp.maximum(size - 1 - 2 * d, 2 * d - size + 1)
    reach = jnp.minimum(d, size - 1 - d)
    far = jnp.where(2 * d < size - 1, size - 1 - k, k)
    pair = jnp.maximum(k - surplus, 0)
    near = d + (1 - 2 * lax.rem(pair, 2)) * (reach - lax.div(pair, 2))
    return jnp.where(k < surplus, far, near)


def send(src, dst, send_sem, recv_sem, axis, peer):
    return pltpu.make_async_remote_copy(
        src_ref=src,
        dst_ref=dst,
        send_sem=send_sem,
        recv_sem=recv_sem,
        device_id={axis: peer},
        device_id_type=MESH,
    )


def kernel(
    net_size,
    dp_size,
    part_hbm,
    assign_hbm,
    img_hbm,
    neg_hbm,
    loss_ref,
    net_grad_ref,
    img_grad_ref,
    img_raw,
    neg_ref,
    part_all,
    assign_all,
    img_all,
    pooled,
    counted,
    unit,
    weights,
    soft,
    tot_all,
    total,
    row_out,
    row_in,
    col_out,
    col_in,
    local_sem,
    part_s,
    part_r,
    fwd_s,
    asg_s,
    asg_r,
    img_s,
    img_r,
    tot_s,
    tot_r,
    row_s,
    row_r,
    col_s,
    col_r,
):
    f32, bf16 = jnp.float32, jnp.bfloat16
    rows = img_raw.shape[0]
    part_rows = part_all.shape[1]
    chunk = part_rows // CHUNKS
    pair_dp = rows * net_size
    row_blocks = pair_dp // BLOCK
    own_blocks = rows // BLOCK
    chips = net_size // 2

    n = lax.axis_index("net")
    d = lax.axis_index("dp")
    core = lax.rem(n, 2)
    chip = lax.div(n, 2)
    sibling = n + 1 - 2 * core

    def net_peer(k):
        return lax.rem(n + k, net_size)

    def dp_peer(k):
        return line_peer(k - 1, d, dp_size)

    def chip_peer(k):
        return lax.rem(chip + k, chips)

    img_load = pltpu.make_async_copy(img_hbm, img_raw, local_sem.at[0])
    part_load = pltpu.make_async_copy(part_hbm, part_all.at[n], local_sem.at[1])
    asg_load = pltpu.make_async_copy(assign_hbm, assign_all.at[n], local_sem.at[2])
    neg_load = pltpu.make_async_copy(neg_hbm, neg_ref, local_sem.at[3])

    barrier = pltpu.get_barrier_semaphore()
    each(
        net_size,
        lambda k: pl.semaphore_signal(
            barrier, inc=1, device_id={"net": net_peer(k)}, device_id_type=MESH
        ),
    )
    each(
        dp_size,
        lambda k: pl.semaphore_signal(
            barrier, inc=1, device_id={"dp": dp_peer(k)}, device_id_type=MESH
        ),
    )

    img_load.start()
    part_load.start()
    asg_load.start()
    neg_load.start()
    img_load.wait()
    h = img_raw[...].astype(f32)
    squares = jnp.sum(h * h, axis=1, keepdims=True)
    img_all[d] = (h * lax.rsqrt(squares + 1e-06)).astype(bf16)

    pl.semaphore_wait(barrier, net_size + dp_size - 2)

    def img_copy(k):
        return send(
            img_all.at[d], img_all.at[d], img_s.at[k], img_r.at[d], "dp", dp_peer(k)
        )

    def img_arrival(src):
        return send(img_all.at[src], img_all.at[src], img_s.at[0], img_r.at[src], "dp", d)

    def part_piece(ref, c):
        return ref.at[pl.ds(c * chunk, chunk)]

    def part_cross(k, c):
        return send(
            part_piece(part_hbm, c),
            part_piece(part_all.at[n], c),
            part_s.at[k, c],
            part_r.at[n, c],
            "net",
            chip_peer(k) * 2 + core,
        )

    def part_sibling(c):
        return send(
            part_piece(part_hbm, c),
            part_piece(part_all.at[n], c),
            part_s.at[0, c],
            part_r.at[n, c],
            "net",
            sibling,
        )

    def part_forward(k, c):
        origin = chip_peer(k) * 2 + core
        return send(
            part_piece(part_all.at[origin], c),
            part_piece(part_all.at[origin], c),
            fwd_s.at[k, c],
            part_r.at[origin, c],
            "net",
            sibling,
        )

    def part_arrival(origin, c):
        return send(
            part_piece(part_all.at[origin], c),
            part_piece(part_all.at[origin], c),
            part_s.at[0, c],
            part_r.at[origin, c],
            "net",
            sibling,
        )

    def asg_copy(k):
        return send(
            assign_hbm, assign_all.at[n], asg_s.at[k], asg_r.at[n], "net", net_peer(k)
        )

    def asg_arrival(src):
        return send(
            assign_hbm, assign_all.at[src], asg_s.at[0], asg_r.at[src], "net", sibling
        )

    each(net_size, lambda k: asg_copy(k).start())
    for c in range(CHUNKS):
        each(chips, lambda k: part_cross(k, c).start())
    each(dp_size, lambda k: img_copy(k).start())
    for c in range(CHUNKS):
        part_sibling(c).start()

    pair_ids = d * pair_dp + lax.broadcasted_iota(jnp.int32, (pair_dp, part_rows), 0)

    def pool(origin, assigned, first=False):
        member = (assigned == pair_ids).astype(f32)
        sums = jnp.dot(member.astype(bf16), part_all[origin], preferred_element_type=f32)
        counts = jnp.sum(member, axis=1, keepdims=True)
        if first:
            pooled[...] = sums
            counted[...] = counts
        else:
            pooled[...] += sums
            counted[...] += counts

    part_load.wait()
    asg_load.wait()
    pool(n, assign_all[n], first=True)

    def pool_from(origin):
        asg_arrival(origin).wait_recv()
        pool(origin, assign_all[origin])

    for c in range(CHUNKS):
        part_arrival(sibling, c).wait_recv()
    pool_from(sibling)

    def pass_on(k):
        origin = chip_peer(k) * 2 + core
        for c in range(CHUNKS):
            part_arrival(origin, c).wait_recv()
            part_forward(k, c).start()
        pool_from(origin)

    each(chips, pass_on)

    def pool_passed(k):
        origin = chip_peer(k) * 2 + 1 - core
        for c in range(CHUNKS):
            part_arrival(origin, c).wait_recv()
        pool_from(origin)

    each(chips, pool_passed)

    p = pooled[...]
    cnt = counted[...]
    unit[...] = (
        p * lax.rsqrt(jnp.sum(p * p, axis=1, keepdims=True) + 1e-06 * (cnt * cnt))
    ).astype(bf16)

    def score(src):
        logits = logit_scale * lax.dot_general(
            img_all[src],
            unit[...],
            (((1,), (1,)), ((), ())),
            preferred_element_type=f32,
        )
        w = jnp.exp(logits)
        for q in range(own_blocks):
            column = (src * net_size + n) * own_blocks + q
            marks = []
            for b in range(row_blocks):
                row = d * row_blocks + b
                live = jnp.maximum(neg_ref[row, column], (row == column).astype(jnp.int32))
                marks.append(jnp.full((1, BLOCK), live.astype(f32), f32))
            masked = w[q * BLOCK : (q + 1) * BLOCK] * jnp.concatenate(marks, axis=1)
            start = pl.multiple_of(src * rows + q * BLOCK, BLOCK)
            weights[pl.ds(start, BLOCK), :] = masked
            tot_all[n] += jnp.sum(masked, axis=0, keepdims=True)

    neg_load.wait()
    tot_all[n] = jnp.zeros_like(tot_all[n])
    score(d)

    def score_from(k):
        src = dp_peer(dp_size - k)
        img_arrival(src).wait_recv()
        score(src)

    each(dp_size, score_from)

    def tot_copy(k):
        return send(
            tot_all.at[n], tot_all.at[n], tot_s.at[k], tot_r.at[n], "net", net_peer(k)
        )

    def tot_arrival(src):
        return send(tot_all.at[src], tot_all.at[src], tot_s.at[0], tot_r.at[src], "net", sibling)

    each(net_size, lambda k: tot_copy(k).start())
    total[...] = tot_all[n]

    own = pl.ds(pl.multiple_of(n * rows, BLOCK), rows)
    own_logits = logit_scale * lax.dot_general(
        img_all[d], unit[own, :], (((1,), (1,)), ((), ())), preferred_element_type=f32
    )
    on_diagonal = lax.broadcasted_iota(jnp.int32, (rows, rows), 0) == lax.broadcasted_iota(
        jnp.int32, (rows, rows), 1
    )
    own_logit = jnp.sum(jnp.where(on_diagonal, own_logits, 0.0), axis=0, keepdims=True)

    def add_total(k):
        src = net_peer(k)
        tot_arrival(src).wait_recv()
        total[...] += tot_all[src]

    each(net_size, add_total)
    inverse = 1.0 / total[...]
    loss_ref[...] = jnp.log(total[:, own]) - own_logit

    def column_grad(src):
        span = pl.ds(pl.multiple_of(src * rows, BLOCK), rows)
        s = (weights[span, :] * inverse).astype(bf16)
        soft[span, :] = s
        return jnp.dot(s, unit[...], preferred_element_type=f32)

    def col_copy(k):
        peer = dp_peer(k)
        return send(
            col_out.at[peer], col_in.at[d], col_s.at[k], col_r.at[d], "dp", peer
        )

    def col_arrival(src):
        return send(col_out.at[src], col_in.at[src], col_s.at[0], col_r.at[src], "dp", d)

    def column_send(k):
        peer = dp_peer(k)
        col_out[peer] = column_grad(peer).astype(bf16)
        col_copy(k).start()

    each(dp_size, column_send)
    img_grad_ref[...] = column_grad(d) - unit[own, :].astype(f32)

    every_image = img_all[...].reshape(dp_size * rows, img_all.shape[2])

    def row_grad(dst):
        span = pl.ds(pl.multiple_of(dst * rows, BLOCK), rows)
        return lax.dot_general(
            soft[:, span], every_image, (((0,), (0,)), ((), ())), preferred_element_type=f32
        )

    def row_copy(k):
        peer = net_peer(k)
        return send(row_out.at[peer], row_in.at[n], row_s.at[k], row_r.at[n], "net", peer)

    def row_arrival(src):
        return send(row_out.at[src], row_in.at[src], row_s.at[0], row_r.at[src], "net", sibling)

    def row_send(k):
        peer = net_peer(k)
        row_out[peer] = row_grad(peer).astype(bf16)
        row_copy(k).start()

    each(net_size, row_send)
    net_grad_ref[...] = row_grad(n) - img_all[d].astype(f32)

    def row_add(k):
        src = net_peer(k)
        row_arrival(src).wait_recv()
        net_grad_ref[...] += row_in[src].astype(f32)

    each(net_size, row_add)
    net_grad_ref[...] = logit_scale * net_grad_ref[...]

    def col_add(k):
        src = dp_peer(dp_size - k)
        col_arrival(src).wait_recv()
        img_grad_ref[...] += col_in[src].astype(f32)

    each(dp_size, col_add)
    img_grad_ref[...] = logit_scale * img_grad_ref[...]

    def net_done(k):
        asg_copy(k).wait_send()
        tot_copy(k).wait_send()
        row_copy(k).wait_send()

    def dp_done(k):
        img_copy(k).wait_send()
        col_copy(k).wait_send()

    each(net_size, net_done)
    each(dp_size, dp_done)
    for c in range(CHUNKS):
        part_sibling(c).wait_send()

        def chip_done(k):
            part_cross(k, c).wait_send()
            part_forward(k, c).wait_send()

        each(chips, chip_done)


def hand_over(loss, net_grad, img_grad, loss_out, net_out, img_out, sem):
    copies = [
        pltpu.make_async_copy(src, dst, sem.at[i])
        for i, (src, dst) in enumerate(
            ((loss, loss_out), (net_grad, net_out), (img_grad, img_out))
        )
    ]
    for copy in copies:
        copy.start()
    for copy in copies:
        copy.wait()


def per_device(part_emb, assign, images, negatives):
    rows, width = images.shape
    part_rows = part_emb.shape[0]
    net_size = lax.axis_size("net")
    dp_size = lax.axis_size("dp")
    chips = net_size // 2
    pair_dp = rows * net_size
    columns = rows * dp_size
    f32, bf16 = jnp.float32, jnp.bfloat16
    dma = pltpu.SemaphoreType.DMA
    vmem = pl.BlockSpec(memory_space=pltpu.VMEM)
    hbm = pl.BlockSpec(memory_space=pltpu.HBM)
    results = (
        jax.ShapeDtypeStruct((1, rows), f32),
        jax.ShapeDtypeStruct((rows, width), f32),
        jax.ShapeDtypeStruct((rows, width), f32),
    )
    loss, net_grad, img_grad = pl.pallas_call(
        functools.partial(kernel, net_size, dp_size),
        out_shape=results,
        in_specs=[hbm, hbm, hbm, hbm],
        out_specs=(vmem, vmem, vmem),
        scratch_shapes=[
            pltpu.VMEM((rows, width), bf16),
            pltpu.SMEM(negatives.shape, jnp.int32),
            pltpu.VMEM((net_size, part_rows, width), bf16),
            pltpu.VMEM((net_size, 1, part_rows), jnp.int32),
            pltpu.VMEM((dp_size, rows, width), bf16),
            pltpu.VMEM((pair_dp, width), f32),
            pltpu.VMEM((pair_dp, 1), f32),
            pltpu.VMEM((pair_dp, width), bf16),
            pltpu.VMEM((columns, pair_dp), f32),
            pltpu.VMEM((columns, pair_dp), bf16),
            pltpu.VMEM((net_size, 1, pair_dp), f32),
            pltpu.VMEM((1, pair_dp), f32),
            pltpu.VMEM((net_size, rows, width), bf16),
            pltpu.VMEM((net_size, rows, width), bf16),
            pltpu.VMEM((dp_size, rows, width), bf16),
            pltpu.VMEM((dp_size, rows, width), bf16),
            dma((4,)),
            dma((chips, CHUNKS)),
            dma((net_size, CHUNKS)),
            dma((chips, CHUNKS)),
            dma((net_size,)),
            dma((net_size,)),
            dma((dp_size,)),
            dma((dp_size,)),
            dma((net_size,)),
            dma((net_size,)),
            dma((net_size,)),
            dma((net_size,)),
            dma((dp_size,)),
            dma((dp_size,)),
        ],
        compiler_params=pltpu.CompilerParams(
            collective_id=0, has_side_effects=True, vmem_limit_bytes=48 * 2**20
        ),
    )(*(
        pltpu.with_memory_space_constraint(array, pltpu.HBM)
        for array in (part_emb, assign.reshape(1, part_rows), images, negatives)
    ))
    loss, net_grad, img_grad = pl.pallas_call(
        hand_over,
        out_shape=results,
        in_specs=[vmem] * 3,
        out_specs=(hbm, hbm, hbm),
        scratch_shapes=[dma((3,))],
    )(*(
        pltpu.with_memory_space_constraint(array, pltpu.VMEM)
        for array in (loss, net_grad, img_grad)
    ))
    return loss.reshape(rows), net_grad, img_grad


def solution(mesh):
    in_specs = (
        P(("groups", "dp", "net"), None),
        P(("groups", "dp", "net")),
        P(("groups", "dp", "net"), None),
        P("groups", None),
    )
    out_specs = (
        P(("groups", "dp", "net")),
        P(("groups", "dp", "net"), None),
        P(("groups", "dp", "net"), None),
    )
    return jax.shard_map(
        per_device, mesh=mesh, in_specs=in_specs, out_specs=out_specs, check_vma=False
    )
```

```python
import functools

import jax
import jax.numpy as jnp
from jax import lax
from jax.experimental import pallas as pl
from jax.experimental.pallas import tpu as pltpu
from jax.sharding import PartitionSpec as P

BLOCK = 128
CHUNKS = 2
MESH = pl.DeviceIdType.MESH

logit_scale = 10.0


def each(count, body):
    if count <= 4:
        for k in range(1, count):
            body(k)
    else:

        def step(k, carry):
            body(k)
            return carry

        lax.fori_loop(1, count, step, 0)


def line_peer(k, d, size):
    surplus = jnp.maximum(size - 1 - 2 * d, 2 * d - size + 1)
    reach = jnp.minimum(d, size - 1 - d)
    far = jnp.where(2 * d < size - 1, size - 1 - k, k)
    pair = jnp.maximum(k - surplus, 0)
    near = d + (1 - 2 * lax.rem(pair, 2)) * (reach - lax.div(pair, 2))
    return jnp.where(k < surplus, far, near)


def send(src, dst, send_sem, recv_sem, axis, peer):
    return pltpu.make_async_remote_copy(
        src_ref=src,
        dst_ref=dst,
        send_sem=send_sem,
        recv_sem=recv_sem,
        device_id={axis: peer},
        device_id_type=MESH,
    )


def kernel(
    net_size,
    dp_size,
    part_hbm,
    assign_hbm,
    img_hbm,
    neg_hbm,
    loss_ref,
    net_grad_ref,
    img_grad_ref,
    img_raw,
    neg_ref,
    part_all,
    assign_all,
    img_all,
    pooled,
    counted,
    unit,
    weights,
    soft,
    tot_all,
    total,
    row_out,
    row_in,
    col_out,
    col_in,
    local_sem,
    part_s,
    part_r,
    fwd_s,
    asg_s,
    asg_r,
    img_s,
    img_r,
    tot_s,
    tot_r,
    row_s,
    row_r,
    col_s,
    col_r,
    held,
    relay_in,
    relay_s,
    relay_r,
):
    f32, bf16 = jnp.float32, jnp.bfloat16
    rows = img_raw.shape[0]
    part_rows = part_all.shape[1]
    chunk = part_rows // CHUNKS
    pair_dp = rows * net_size
    row_blocks = pair_dp // BLOCK
    own_blocks = rows // BLOCK
    chips = net_size // 2

    n = lax.axis_index("net")
    d = lax.axis_index("dp")
    core = lax.rem(n, 2)
    chip = lax.div(n, 2)
    sibling = n + 1 - 2 * core

    def net_peer(k):
        return lax.rem(n + k, net_size)

    def dp_peer(k):
        return line_peer(k - 1, d, dp_size)

    def chip_peer(k):
        return lax.rem(chip + k, chips)

    img_load = pltpu.make_async_copy(img_hbm, img_raw, local_sem.at[0])
    part_load = pltpu.make_async_copy(part_hbm, part_all.at[n], local_sem.at[1])
    asg_load = pltpu.make_async_copy(assign_hbm, assign_all.at[n], local_sem.at[2])
    neg_load = pltpu.make_async_copy(neg_hbm, neg_ref, local_sem.at[3])

    barrier = pltpu.get_barrier_semaphore()
    each(
        net_size,
        lambda k: pl.semaphore_signal(
            barrier, inc=1, device_id={"net": net_peer(k)}, device_id_type=MESH
        ),
    )
    each(
        dp_size,
        lambda k: pl.semaphore_signal(
            barrier, inc=1, device_id={"dp": dp_peer(k)}, device_id_type=MESH
        ),
    )

    img_load.start()
    part_load.start()
    asg_load.start()
    neg_load.start()
    img_load.wait()
    h = img_raw[...].astype(f32)
    squares = jnp.sum(h * h, axis=1, keepdims=True)
    img_all[d] = (h * lax.rsqrt(squares + 1e-06)).astype(bf16)

    pl.semaphore_wait(barrier, net_size + dp_size - 2)

    def img_copy(k):
        return send(
            img_all.at[d], img_all.at[d], img_s.at[k], img_r.at[d], "dp", dp_peer(k)
        )

    line = dp_size == 4
    at_end = lax.rem(d, 3) == 0
    in_middle = lax.rem(d, 3) > 0

    def img_start(k):
        if line and k == 1:
            pl.when(in_middle)(lambda: img_copy(k).start())
        else:
            img_copy(k).start()

    def img_relay():
        src = dp_peer(1)
        return send(
            img_all.at[src], img_all.at[src], relay_s, img_r.at[src], "dp", 3 * d - 3
        )

    def img_arrival(src):
        return send(img_all.at[src], img_all.at[src], img_s.at[0], img_r.at[src], "dp", d)

    def part_piece(ref, c):
        return ref.at[pl.ds(c * chunk, chunk)]

    def part_cross(k, c):
        return send(
            part_piece(part_hbm, c),
            part_piece(part_all.at[n], c),
            part_s.at[k, c],
            part_r.at[n, c],
            "net",
            chip_peer(k) * 2 + core,
        )

    def part_sibling(c):
        return send(
            part_piece(part_hbm, c),
            part_piece(part_all.at[n], c),
            part_s.at[0, c],
            part_r.at[n, c],
            "net",
            sibling,
        )

    def part_forward(k, c):
        origin = chip_peer(k) * 2 + core
        return send(
            part_piece(part_all.at[origin], c),
            part_piece(part_all.at[origin], c),
            fwd_s.at[k, c],
            part_r.at[origin, c],
            "net",
            sibling,
        )

    def part_arrival(origin, c):
        return send(
            part_piece(part_all.at[origin], c),
            part_piece(part_all.at[origin], c),
            part_s.at[0, c],
            part_r.at[origin, c],
            "net",
            sibling,
        )

    def asg_copy(k):
        return send(
            assign_hbm, assign_all.at[n], asg_s.at[k], asg_r.at[n], "net", net_peer(k)
        )

    def asg_arrival(src):
        return send(
            assign_hbm, assign_all.at[src], asg_s.at[0], asg_r.at[src], "net", sibling
        )

    each(net_size, lambda k: asg_copy(k).start())
    for c in range(CHUNKS):
        each(chips, lambda k: part_cross(k, c).start())
    each(dp_size, img_start)
    for c in range(CHUNKS):
        part_sibling(c).start()

    pair_ids = d * pair_dp + lax.broadcasted_iota(jnp.int32, (pair_dp, part_rows), 0)

    def pool(origin, assigned, first=False):
        member = (assigned == pair_ids).astype(f32)
        sums = jnp.dot(member.astype(bf16), part_all[origin], preferred_element_type=f32)
        counts = jnp.sum(member, axis=1, keepdims=True)
        if first:
            pooled[...] = sums
            counted[...] = counts
        else:
            pooled[...] += sums
            counted[...] += counts

    part_load.wait()
    asg_load.wait()
    pool(n, assign_all[n], first=True)

    def pool_from(origin):
        asg_arrival(origin).wait_recv()
        pool(origin, assign_all[origin])

    for c in range(CHUNKS):
        part_arrival(sibling, c).wait_recv()
    pool_from(sibling)

    def pass_on(k):
        origin = chip_peer(k) * 2 + core
        for c in range(CHUNKS):
            part_arrival(origin, c).wait_recv()
            part_forward(k, c).start()
        pool_from(origin)

    if line:

        @pl.when(in_middle)
        def _():
            img_arrival(dp_peer(1)).wait_recv()
            img_relay().start()

    each(chips, pass_on)

    def pool_passed(k):
        origin = chip_peer(k) * 2 + 1 - core
        for c in range(CHUNKS):
            part_arrival(origin, c).wait_recv()
        pool_from(origin)

    each(chips, pool_passed)

    p = pooled[...]
    cnt = counted[...]
    unit[...] = (
        p * lax.rsqrt(jnp.sum(p * p, axis=1, keepdims=True) + 1e-06 * (cnt * cnt))
    ).astype(bf16)

    def score(src):
        logits = logit_scale * lax.dot_general(
            img_all[src],
            unit[...],
            (((1,), (1,)), ((), ())),
            preferred_element_type=f32,
        )
        w = jnp.exp(logits)
        for q in range(own_blocks):
            column = (src * net_size + n) * own_blocks + q
            marks = []
            for b in range(row_blocks):
                row = d * row_blocks + b
                live = jnp.maximum(neg_ref[row, column], (row == column).astype(jnp.int32))
                marks.append(jnp.full((1, BLOCK), live.astype(f32), f32))
            masked = w[q * BLOCK : (q + 1) * BLOCK] * jnp.concatenate(marks, axis=1)
            start = pl.multiple_of(src * rows + q * BLOCK, BLOCK)
            weights[pl.ds(start, BLOCK), :] = masked
            tot_all[n] += jnp.sum(masked, axis=0, keepdims=True)

    neg_load.wait()
    tot_all[n] = jnp.zeros_like(tot_all[n])
    score(d)

    def score_from(k):
        src = dp_peer(dp_size - k)
        if line and k == dp_size - 1:
            pl.when(at_end)(lambda: img_arrival(src).wait_recv())
        else:
            img_arrival(src).wait_recv()
        score(src)

    each(dp_size, score_from)

    def tot_copy(k):
        return send(
            tot_all.at[n], tot_all.at[n], tot_s.at[k], tot_r.at[n], "net", net_peer(k)
        )

    def tot_arrival(src):
        return send(tot_all.at[src], tot_all.at[src], tot_s.at[0], tot_r.at[src], "net", sibling)

    each(net_size, lambda k: tot_copy(k).start())
    total[...] = tot_all[n]

    own = pl.ds(pl.multiple_of(n * rows, BLOCK), rows)
    own_logits = logit_scale * lax.dot_general(
        img_all[d], unit[own, :], (((1,), (1,)), ((), ())), preferred_element_type=f32
    )
    on_diagonal = lax.broadcasted_iota(jnp.int32, (rows, rows), 0) == lax.broadcasted_iota(
        jnp.int32, (rows, rows), 1
    )
    own_logit = jnp.sum(jnp.where(on_diagonal, own_logits, 0.0), axis=0, keepdims=True)

    def add_total(k):
        src = net_peer(k)
        tot_arrival(src).wait_recv()
        total[...] += tot_all[src]

    each(net_size, add_total)
    inverse = 1.0 / total[...]
    loss_ref[...] = jnp.log(total[:, own]) - own_logit

    def column_grad(src):
        span = pl.ds(pl.multiple_of(src * rows, BLOCK), rows)
        s = (weights[span, :] * inverse).astype(bf16)
        soft[span, :] = s
        return jnp.dot(s, unit[...], preferred_element_type=f32)

    def col_copy(k):
        peer = dp_peer(k)
        return send(
            col_out.at[peer], col_in.at[d], col_s.at[k], col_r.at[d], "dp", peer
        )

    def col_arrival(src):
        return send(col_out.at[src], col_in.at[src], col_s.at[0], col_r.at[src], "dp", d)

    def col_relay():
        return send(
            col_out.at[dp_peer(1)], relay_in, col_s.at[1], relay_r, "dp", dp_peer(dp_size - 1)
        )

    def column_send(k):
        peer = dp_peer(k)
        sums = column_grad(peer)
        if line and k == 1:

            @pl.when(at_end)
            def _():
                col_out[peer] = sums.astype(bf16)
                col_relay().start()

            @pl.when(in_middle)
            def _():
                held[...] = sums

        else:
            col_out[peer] = sums.astype(bf16)
            col_copy(k).start()

    each(dp_size, column_send)
    img_grad_ref[...] = column_grad(d) - unit[own, :].astype(f32)

    every_image = img_all[...].reshape(dp_size * rows, img_all.shape[2])

    def row_grad(dst):
        span = pl.ds(pl.multiple_of(dst * rows, BLOCK), rows)
        return lax.dot_general(
            soft[:, span], every_image, (((0,), (0,)), ((), ())), preferred_element_type=f32
        )

    def row_copy(k):
        peer = net_peer(k)
        return send(row_out.at[peer], row_in.at[n], row_s.at[k], row_r.at[n], "net", peer)

    def row_arrival(src):
        return send(row_out.at[src], row_in.at[src], row_s.at[0], row_r.at[src], "net", sibling)

    def row_send(k):
        peer = net_peer(k)
        row_out[peer] = row_grad(peer).astype(bf16)
        row_copy(k).start()

    each(net_size, row_send)
    net_grad_ref[...] = row_grad(n) - img_all[d].astype(f32)

    if line:

        @pl.when(in_middle)
        def _():
            col_relay().wait_recv()
            far = dp_peer(1)
            col_out[far] = (held[...] + relay_in[...].astype(f32)).astype(bf16)
            col_copy(1).start()

    def row_add(k):
        src = net_peer(k)
        row_arrival(src).wait_recv()
        net_grad_ref[...] += row_in[src].astype(f32)

    each(net_size, row_add)
    net_grad_ref[...] = logit_scale * net_grad_ref[...]

    def col_add(k):
        src = dp_peer(dp_size - k)

        def add():
            col_arrival(src).wait_recv()
            img_grad_ref[...] += col_in[src].astype(f32)

        if line and k == dp_size - 1:
            pl.when(in_middle)(add)
        else:
            add()

    each(dp_size, col_add)
    img_grad_ref[...] = logit_scale * img_grad_ref[...]

    def net_done(k):
        asg_copy(k).wait_send()
        tot_copy(k).wait_send()
        row_copy(k).wait_send()

    def dp_done(k):
        if line and k == 1:

            @pl.when(in_middle)
            def _():
                img_copy(k).wait_send()
                img_relay().wait_send()

            @pl.when(at_end)
            def _():
                col_relay().wait_send()

            pl.when(in_middle)(lambda: col_copy(k).wait_send())
        else:
            img_copy(k).wait_send()
            col_copy(k).wait_send()

    each(net_size, net_done)
    each(dp_size, dp_done)
    for c in range(CHUNKS):
        part_sibling(c).wait_send()

        def chip_done(k):
            part_cross(k, c).wait_send()
            part_forward(k, c).wait_send()

        each(chips, chip_done)


def hand_over(loss, net_grad, img_grad, loss_out, net_out, img_out, sem):
    copies = [
        pltpu.make_async_copy(src, dst, sem.at[i])
        for i, (src, dst) in enumerate(
            ((loss, loss_out), (net_grad, net_out), (img_grad, img_out))
        )
    ]
    for copy in copies:
        copy.start()
    for copy in copies:
        copy.wait()


def per_device(part_emb, assign, images, negatives):
    rows, width = images.shape
    part_rows = part_emb.shape[0]
    net_size = lax.axis_size("net")
    dp_size = lax.axis_size("dp")
    chips = net_size // 2
    pair_dp = rows * net_size
    columns = rows * dp_size
    f32, bf16 = jnp.float32, jnp.bfloat16
    dma = pltpu.SemaphoreType.DMA
    vmem = pl.BlockSpec(memory_space=pltpu.VMEM)
    hbm = pl.BlockSpec(memory_space=pltpu.HBM)
    results = (
        jax.ShapeDtypeStruct((1, rows), f32),
        jax.ShapeDtypeStruct((rows, width), f32),
        jax.ShapeDtypeStruct((rows, width), f32),
    )
    loss, net_grad, img_grad = pl.pallas_call(
        functools.partial(kernel, net_size, dp_size),
        out_shape=results,
        in_specs=[hbm, hbm, hbm, hbm],
        out_specs=(vmem, vmem, vmem),
        scratch_shapes=[
            pltpu.VMEM((rows, width), bf16),
            pltpu.SMEM(negatives.shape, jnp.int32),
            pltpu.VMEM((net_size, part_rows, width), bf16),
            pltpu.VMEM((net_size, 1, part_rows), jnp.int32),
            pltpu.VMEM((dp_size, rows, width), bf16),
            pltpu.VMEM((pair_dp, width), f32),
            pltpu.VMEM((pair_dp, 1), f32),
            pltpu.VMEM((pair_dp, width), bf16),
            pltpu.VMEM((columns, pair_dp), f32),
            pltpu.VMEM((columns, pair_dp), bf16),
            pltpu.VMEM((net_size, 1, pair_dp), f32),
            pltpu.VMEM((1, pair_dp), f32),
            pltpu.VMEM((net_size, rows, width), bf16),
            pltpu.VMEM((net_size, rows, width), bf16),
            pltpu.VMEM((dp_size, rows, width), bf16),
            pltpu.VMEM((dp_size, rows, width), bf16),
            dma((4,)),
            dma((chips, CHUNKS)),
            dma((net_size, CHUNKS)),
            dma((chips, CHUNKS)),
            dma((net_size,)),
            dma((net_size,)),
            dma((dp_size,)),
            dma((dp_size,)),
            dma((net_size,)),
            dma((net_size,)),
            dma((net_size,)),
            dma((net_size,)),
            dma((dp_size,)),
            dma((dp_size,)),
            pltpu.VMEM((rows, width), f32),
            pltpu.VMEM((rows, width), bf16),
            dma(()),
            dma(()),
        ],
        compiler_params=pltpu.CompilerParams(
            collective_id=0, has_side_effects=True, vmem_limit_bytes=48 * 2**20
        ),
    )(*(
        pltpu.with_memory_space_constraint(array, pltpu.HBM)
        for array in (part_emb, assign.reshape(1, part_rows), images, negatives)
    ))
    loss, net_grad, img_grad = pl.pallas_call(
        hand_over,
        out_shape=results,
        in_specs=[vmem] * 3,
        out_specs=(hbm, hbm, hbm),
        scratch_shapes=[dma((3,))],
    )(*(
        pltpu.with_memory_space_constraint(array, pltpu.VMEM)
        for array in (loss, net_grad, img_grad)
    ))
    return loss.reshape(rows), net_grad, img_grad


def solution(mesh):
    in_specs = (
        P(("groups", "dp", "net"), None),
        P(("groups", "dp", "net")),
        P(("groups", "dp", "net"), None),
        P("groups", None),
    )
    out_specs = (
        P(("groups", "dp", "net")),
        P(("groups", "dp", "net"), None),
        P(("groups", "dp", "net"), None),
    )
    return jax.shard_map(
        per_device, mesh=mesh, in_specs=in_specs, out_specs=out_specs, check_vma=False
    )
```

```python
import functools

import jax
import jax.numpy as jnp
from jax import lax
from jax.experimental import pallas as pl
from jax.experimental.pallas import tpu as pltpu
from jax.sharding import PartitionSpec as P

BLOCK = 128
CHUNKS = 2
MESH = pl.DeviceIdType.MESH

logit_scale = 10.0


def each(count, body):
    if count <= 4:
        for k in range(1, count):
            body(k)
    else:

        def step(k, carry):
            body(k)
            return carry

        lax.fori_loop(1, count, step, 0)


def line_peer(k, d, size):
    surplus = jnp.maximum(size - 1 - 2 * d, 2 * d - size + 1)
    reach = jnp.minimum(d, size - 1 - d)
    far = jnp.where(2 * d < size - 1, size - 1 - k, k)
    pair = jnp.maximum(k - surplus, 0)
    near = d + (1 - 2 * lax.rem(pair, 2)) * (reach - lax.div(pair, 2))
    return jnp.where(k < surplus, far, near)


def send(src, dst, send_sem, recv_sem, axis, peer):
    return pltpu.make_async_remote_copy(
        src_ref=src,
        dst_ref=dst,
        send_sem=send_sem,
        recv_sem=recv_sem,
        device_id={axis: peer},
        device_id_type=MESH,
    )


def kernel(
    net_size,
    dp_size,
    part_hbm,
    assign_hbm,
    img_hbm,
    neg_hbm,
    loss_ref,
    net_grad_ref,
    img_grad_ref,
    img_raw,
    neg_ref,
    part_all,
    assign_all,
    img_all,
    pooled,
    counted,
    unit,
    weights,
    soft,
    tot_all,
    total,
    row_out,
    row_in,
    col_out,
    col_in,
    local_sem,
    part_s,
    part_r,
    fwd_s,
    asg_s,
    asg_r,
    img_s,
    img_r,
    tot_s,
    tot_r,
    row_s,
    row_r,
    col_s,
    col_r,
    held,
    relay_in,
    relay_s,
    relay_r,
):
    f32, bf16 = jnp.float32, jnp.bfloat16
    rows = img_raw.shape[0]
    part_rows = part_all.shape[1]
    chunk = part_rows // CHUNKS
    pair_dp = rows * net_size
    row_blocks = pair_dp // BLOCK
    own_blocks = rows // BLOCK
    chips = net_size // 2

    n = lax.axis_index("net")
    d = lax.axis_index("dp")
    core = lax.rem(n, 2)
    chip = lax.div(n, 2)
    sibling = n + 1 - 2 * core

    def net_peer(k):
        return lax.rem(n + k, net_size)

    def dp_peer(k):
        return line_peer(k - 1, d, dp_size)

    def chip_peer(k):
        return lax.rem(chip + k, chips)

    img_load = pltpu.make_async_copy(img_hbm, img_raw, local_sem.at[0])
    part_load = pltpu.make_async_copy(part_hbm, part_all.at[n], local_sem.at[1])
    asg_load = pltpu.make_async_copy(assign_hbm, assign_all.at[n], local_sem.at[2])
    neg_load = pltpu.make_async_copy(neg_hbm, neg_ref, local_sem.at[3])

    barrier = pltpu.get_barrier_semaphore()
    each(
        net_size,
        lambda k: pl.semaphore_signal(
            barrier, inc=1, device_id={"net": net_peer(k)}, device_id_type=MESH
        ),
    )
    each(
        dp_size,
        lambda k: pl.semaphore_signal(
            barrier, inc=1, device_id={"dp": dp_peer(k)}, device_id_type=MESH
        ),
    )

    img_load.start()
    part_load.start()
    asg_load.start()
    neg_load.start()
    img_load.wait()
    h = img_raw[...].astype(f32)
    squares = jnp.sum(h * h, axis=1, keepdims=True)
    img_all[d] = (h * lax.rsqrt(squares + 1e-06)).astype(bf16)

    pl.semaphore_wait(barrier, net_size + dp_size - 2)

    def img_copy(k):
        return send(
            img_all.at[d], img_all.at[d], img_s.at[k], img_r.at[d], "dp", dp_peer(k)
        )

    line = dp_size == 4
    at_end = lax.rem(d, 3) == 0
    in_middle = lax.rem(d, 3) > 0

    def img_start(k):
        if line and k == 1:
            pl.when(in_middle)(lambda: img_copy(k).start())
        else:
            img_copy(k).start()

    def img_relay():
        src = dp_peer(1)
        return send(
            img_all.at[src], img_all.at[src], relay_s, img_r.at[src], "dp", 3 * d - 3
        )

    def img_arrival(src):
        return send(img_all.at[src], img_all.at[src], img_s.at[0], img_r.at[src], "dp", d)

    def part_piece(ref, c):
        return ref.at[pl.ds(c * chunk, chunk)]

    def part_cross(k, c):
        return send(
            part_piece(part_hbm, c),
            part_piece(part_all.at[n], c),
            part_s.at[k, c],
            part_r.at[n, c],
            "net",
            chip_peer(k) * 2 + core,
        )

    def part_sibling(c):
        return send(
            part_piece(part_hbm, c),
            part_piece(part_all.at[n], c),
            part_s.at[0, c],
            part_r.at[n, c],
            "net",
            sibling,
        )

    def part_forward(k, c):
        origin = chip_peer(k) * 2 + core
        return send(
            part_piece(part_all.at[origin], c),
            part_piece(part_all.at[origin], c),
            fwd_s.at[k, c],
            part_r.at[origin, c],
            "net",
            sibling,
        )

    def part_arrival(origin, c):
        return send(
            part_piece(part_all.at[origin], c),
            part_piece(part_all.at[origin], c),
            part_s.at[0, c],
            part_r.at[origin, c],
            "net",
            sibling,
        )

    def asg_copy(k):
        return send(
            assign_hbm, assign_all.at[n], asg_s.at[k], asg_r.at[n], "net", net_peer(k)
        )

    def asg_arrival(src):
        return send(
            assign_hbm, assign_all.at[src], asg_s.at[0], asg_r.at[src], "net", sibling
        )

    each(net_size, lambda k: asg_copy(k).start())
    for c in range(CHUNKS):
        each(chips, lambda k: part_cross(k, c).start())
    each(dp_size, img_start)
    for c in range(CHUNKS):
        part_sibling(c).start()

    pair_ids = d * pair_dp + lax.broadcasted_iota(jnp.int32, (pair_dp, part_rows), 0)

    def pool(origin, assigned, first=False):
        member = (assigned == pair_ids).astype(f32)
        sums = jnp.dot(member.astype(bf16), part_all[origin], preferred_element_type=f32)
        counts = jnp.sum(member, axis=1, keepdims=True)
        if first:
            pooled[...] = sums
            counted[...] = counts
        else:
            pooled[...] += sums
            counted[...] += counts

    part_load.wait()
    asg_load.wait()
    pool(n, assign_all[n], first=True)

    def pool_from(origin):
        asg_arrival(origin).wait_recv()
        pool(origin, assign_all[origin])

    for c in range(CHUNKS):
        part_arrival(sibling, c).wait_recv()
    pool_from(sibling)

    def pass_on(k):
        origin = chip_peer(k) * 2 + core
        for c in range(CHUNKS):
            part_arrival(origin, c).wait_recv()
            part_forward(k, c).start()
        pool_from(origin)

    if line:

        @pl.when(in_middle)
        def _():
            img_arrival(dp_peer(1)).wait_recv()
            img_relay().start()

    each(chips, pass_on)

    def pool_passed(k):
        origin = chip_peer(k) * 2 + 1 - core
        for c in range(CHUNKS):
            part_arrival(origin, c).wait_recv()
        pool_from(origin)

    each(chips, pool_passed)

    p = pooled[...]
    cnt = counted[...]
    unit[...] = (
        p * lax.rsqrt(jnp.sum(p * p, axis=1, keepdims=True) + 1e-06 * (cnt * cnt))
    ).astype(bf16)

    def score(src):
        logits = logit_scale * lax.dot_general(
            img_all[src],
            unit[...],
            (((1,), (1,)), ((), ())),
            preferred_element_type=f32,
        )
        w = jnp.exp(logits)
        for q in range(own_blocks):
            column = (src * net_size + n) * own_blocks + q
            marks = []
            for b in range(row_blocks):
                row = d * row_blocks + b
                live = jnp.maximum(neg_ref[row, column], (row == column).astype(jnp.int32))
                marks.append(jnp.full((1, BLOCK), live.astype(f32), f32))
            masked = w[q * BLOCK : (q + 1) * BLOCK] * jnp.concatenate(marks, axis=1)
            start = pl.multiple_of(src * rows + q * BLOCK, BLOCK)
            weights[pl.ds(start, BLOCK), :] = masked
            tot_all[n] += jnp.sum(masked, axis=0, keepdims=True)

    neg_load.wait()
    tot_all[n] = jnp.zeros_like(tot_all[n])
    score(d)

    def score_from(k):
        src = dp_peer(dp_size - k)
        if line and k == dp_size - 1:
            pl.when(at_end)(lambda: img_arrival(src).wait_recv())
        else:
            img_arrival(src).wait_recv()
        score(src)

    each(dp_size, score_from)

    def tot_copy(k):
        return send(
            tot_all.at[n], tot_all.at[n], tot_s.at[k], tot_r.at[n], "net", net_peer(k)
        )

    def tot_arrival(src):
        return send(tot_all.at[src], tot_all.at[src], tot_s.at[0], tot_r.at[src], "net", sibling)

    each(net_size, lambda k: tot_copy(k).start())
    total[...] = tot_all[n]

    own = pl.ds(pl.multiple_of(n * rows, BLOCK), rows)
    own_logits = logit_scale * lax.dot_general(
        img_all[d], unit[own, :], (((1,), (1,)), ((), ())), preferred_element_type=f32
    )
    on_diagonal = lax.broadcasted_iota(jnp.int32, (rows, rows), 0) == lax.broadcasted_iota(
        jnp.int32, (rows, rows), 1
    )
    own_logit = jnp.sum(jnp.where(on_diagonal, own_logits, 0.0), axis=0, keepdims=True)

    def add_total(k):
        src = net_peer(k)
        tot_arrival(src).wait_recv()
        total[...] += tot_all[src]

    each(net_size, add_total)
    inverse = 1.0 / total[...]
    loss_ref[...] = jnp.log(total[:, own]) - own_logit

    def column_grad(src):
        span = pl.ds(pl.multiple_of(src * rows, BLOCK), rows)
        s = (weights[span, :] * inverse).astype(bf16)
        soft[span, :] = s
        return jnp.dot(s, unit[...], preferred_element_type=f32)

    def col_copy(k):
        peer = dp_peer(k)
        return send(
            col_out.at[peer], col_in.at[d], col_s.at[k], col_r.at[d], "dp", peer
        )

    def col_arrival(src):
        return send(col_out.at[src], col_in.at[src], col_s.at[0], col_r.at[src], "dp", d)

    def col_relay():
        return send(
            col_out.at[dp_peer(1)], relay_in, col_s.at[1], relay_r, "dp", dp_peer(dp_size - 1)
        )

    def column_send(k):
        peer = dp_peer(k)
        sums = column_grad(peer)
        if line and k == 1:

            @pl.when(at_end)
            def _():
                col_out[peer] = sums.astype(bf16)
                col_relay().start()

            @pl.when(in_middle)
            def _():
                held[...] = sums

        else:
            col_out[peer] = sums.astype(bf16)
            if line and k == 2:
                pl.when(at_end)(lambda: col_relay().wait_send())
            col_copy(k).start()

    each(dp_size, column_send)
    img_grad_ref[...] = column_grad(d) - unit[own, :].astype(f32)

    every_image = img_all[...].reshape(dp_size * rows, img_all.shape[2])

    def row_grad(dst):
        span = pl.ds(pl.multiple_of(dst * rows, BLOCK), rows)
        return lax.dot_general(
            soft[:, span], every_image, (((0,), (0,)), ((), ())), preferred_element_type=f32
        )

    def row_copy(k):
        peer = net_peer(k)
        return send(row_out.at[peer], row_in.at[n], row_s.at[k], row_r.at[n], "net", peer)

    def row_arrival(src):
        return send(row_out.at[src], row_in.at[src], row_s.at[0], row_r.at[src], "net", sibling)

    def row_send(k):
        peer = net_peer(k)
        row_out[peer] = row_grad(peer).astype(bf16)
        row_copy(k).start()

    each(net_size, row_send)
    net_grad_ref[...] = row_grad(n) - img_all[d].astype(f32)

    if line:

        @pl.when(in_middle)
        def _():
            col_relay().wait_recv()
            far = dp_peer(1)
            col_out[far] = (held[...] + relay_in[...].astype(f32)).astype(bf16)
            col_copy(1).start()

    def row_add(k):
        src = net_peer(k)
        row_arrival(src).wait_recv()
        net_grad_ref[...] += row_in[src].astype(f32)

    each(net_size, row_add)
    net_grad_ref[...] = logit_scale * net_grad_ref[...]

    def col_add(k):
        src = dp_peer(dp_size - k)

        def add():
            col_arrival(src).wait_recv()
            img_grad_ref[...] += col_in[src].astype(f32)

        if line and k == dp_size - 1:
            pl.when(in_middle)(add)
        else:
            add()

    each(dp_size, col_add)
    img_grad_ref[...] = logit_scale * img_grad_ref[...]

    def net_done(k):
        asg_copy(k).wait_send()
        tot_copy(k).wait_send()
        row_copy(k).wait_send()

    def dp_done(k):
        if line and k == 1:

            @pl.when(in_middle)
            def _():
                img_copy(k).wait_send()
                img_relay().wait_send()

            pl.when(in_middle)(lambda: col_copy(k).wait_send())
        else:
            img_copy(k).wait_send()
            col_copy(k).wait_send()

    each(net_size, net_done)
    each(dp_size, dp_done)
    for c in range(CHUNKS):
        part_sibling(c).wait_send()

        def chip_done(k):
            part_cross(k, c).wait_send()
            part_forward(k, c).wait_send()

        each(chips, chip_done)


def hand_over(loss, net_grad, img_grad, loss_out, net_out, img_out, sem):
    copies = [
        pltpu.make_async_copy(src, dst, sem.at[i])
        for i, (src, dst) in enumerate(
            ((loss, loss_out), (net_grad, net_out), (img_grad, img_out))
        )
    ]
    for copy in copies:
        copy.start()
    for copy in copies:
        copy.wait()


def per_device(part_emb, assign, images, negatives):
    rows, width = images.shape
    part_rows = part_emb.shape[0]
    net_size = lax.axis_size("net")
    dp_size = lax.axis_size("dp")
    chips = net_size // 2
    pair_dp = rows * net_size
    columns = rows * dp_size
    f32, bf16 = jnp.float32, jnp.bfloat16
    dma = pltpu.SemaphoreType.DMA
    vmem = pl.BlockSpec(memory_space=pltpu.VMEM)
    hbm = pl.BlockSpec(memory_space=pltpu.HBM)
    results = (
        jax.ShapeDtypeStruct((1, rows), f32),
        jax.ShapeDtypeStruct((rows, width), f32),
        jax.ShapeDtypeStruct((rows, width), f32),
    )
    loss, net_grad, img_grad = pl.pallas_call(
        functools.partial(kernel, net_size, dp_size),
        out_shape=results,
        in_specs=[hbm, hbm, hbm, hbm],
        out_specs=(vmem, vmem, vmem),
        scratch_shapes=[
            pltpu.VMEM((rows, width), bf16),
            pltpu.SMEM(negatives.shape, jnp.int32),
            pltpu.VMEM((net_size, part_rows, width), bf16),
            pltpu.VMEM((net_size, 1, part_rows), jnp.int32),
            pltpu.VMEM((dp_size, rows, width), bf16),
            pltpu.VMEM((pair_dp, width), f32),
            pltpu.VMEM((pair_dp, 1), f32),
            pltpu.VMEM((pair_dp, width), bf16),
            pltpu.VMEM((columns, pair_dp), f32),
            pltpu.VMEM((columns, pair_dp), bf16),
            pltpu.VMEM((net_size, 1, pair_dp), f32),
            pltpu.VMEM((1, pair_dp), f32),
            pltpu.VMEM((net_size, rows, width), bf16),
            pltpu.VMEM((net_size, rows, width), bf16),
            pltpu.VMEM((dp_size, rows, width), bf16),
            pltpu.VMEM((dp_size, rows, width), bf16),
            dma((4,)),
            dma((chips, CHUNKS)),
            dma((net_size, CHUNKS)),
            dma((chips, CHUNKS)),
            dma((net_size,)),
            dma((net_size,)),
            dma((dp_size,)),
            dma((dp_size,)),
            dma((net_size,)),
            dma((net_size,)),
            dma((net_size,)),
            dma((net_size,)),
            dma((dp_size,)),
            dma((dp_size,)),
            pltpu.VMEM((rows, width), f32),
            pltpu.VMEM((rows, width), bf16),
            dma(()),
            dma(()),
        ],
        compiler_params=pltpu.CompilerParams(
            collective_id=0, has_side_effects=True, vmem_limit_bytes=48 * 2**20
        ),
    )(*(
        pltpu.with_memory_space_constraint(array, pltpu.HBM)
        for array in (part_emb, assign.reshape(1, part_rows), images, negatives)
    ))
    loss, net_grad, img_grad = pl.pallas_call(
        hand_over,
        out_shape=results,
        in_specs=[vmem] * 3,
        out_specs=(hbm, hbm, hbm),
        scratch_shapes=[dma((3,))],
    )(*(
        pltpu.with_memory_space_constraint(array, pltpu.VMEM)
        for array in (loss, net_grad, img_grad)
    ))
    return loss.reshape(rows), net_grad, img_grad


def solution(mesh):
    in_specs = (
        P(("groups", "dp", "net"), None),
        P(("groups", "dp", "net")),
        P(("groups", "dp", "net"), None),
        P("groups", None),
    )
    out_specs = (
        P(("groups", "dp", "net")),
        P(("groups", "dp", "net"), None),
        P(("groups", "dp", "net"), None),
    )
    return jax.shard_map(
        per_device, mesh=mesh, in_specs=in_specs, out_specs=out_specs, check_vma=False
    )
```
